32 devices in a mesh: section: 2 (over y), fsdp: 16 (over z, x, core).
Axes of the slice: x: 2, y: 2, z: 4, core: 2. Of those that a mesh axis runs over, the one named last changes fastest.
Arguments:
- hidden: bfloat16 [2, 2048, 4608], P('section', 'fsdp'), may hold values from -6 to 6
- gain: bfloat16 [2, 4608], P('section'), may hold values from 0.099609375 to 1.8984375
- key_grad: bfloat16 [2, 2048, 512], P('section', 'fsdp'), may hold values from -6 to 6
- residual_grad: bfloat16 [2, 2048, 4608], P('section', 'fsdp'), may hold values from -6 to 6
- key_weight: bfloat16 [2, 4608, 512], P('section', 'fsdp'), may hold values from -0.09375 to 0.09375
Outputs:
- passed_grad: bfloat16 [2, 2048, 4608], P('section', 'fsdp')
- weight_grad: float32 [2, 4608, 512], P('section', 'fsdp')
The draws below stay inside these ranges and needn't reach their ends.
All inputs are finite; a program needn't handle non-finite values.
Results may differ from the reference program's by a relative error of at most 0.0029.
Values may be sent and summed in bfloat16 or wider, within the bound.
No kernel may reach another device: no remote copies, remote signals or barrier semaphores. Data moves between devices by JAX's collectives and lax.ppermute only.
A program may use at most 64 MiB of HBM per device.

```python
import math
import jax
import jax.numpy as jnp
from jax import lax

D = 4608
KW = 512
TOKENS = 2048
SECTIONS = 2


def with_spikes(array, rng, source, target, shards_of, factor):
    def block_of(position):
        return (jnp.arange(array.shape[position]) // (array.shape[position] // shards_of)).reshape((-1,) + (1,) * (array.ndim - 1 - position))

    near = jax.random.permutation(rng, shards_of)[block_of(target)]
    far = (block_of(target) + shards_of // 2) % shards_of
    return jnp.where((block_of(source) == near) | (block_of(source) == far), factor * array, array)


def block_scale(stream_key, extent, shards, smallest, largest):
    factor_of = 1.0
    for position, parts in shards:
        draws = jax.random.uniform(jax.random.fold_in(jax.random.fold_in(stream_key, 6), position), (parts,), jnp.float32, smallest / len(shards), largest / len(shards))
        factor_of = factor_of * jnp.repeat(jnp.exp(draws), extent[position] // parts).reshape((-1,) + (1,) * (len(extent) - 1 - position))
    return factor_of


def centred(rng, extent, width, bound, shards=(), kind=jnp.bfloat16):
    result = jax.random.normal(rng, extent, jnp.float32) * width
    if len(shards) > 0:
        result = block_scale(rng, extent, shards, -0.22, 0.18) * result
    return jnp.clip(result, min=-bound, max=bound).astype(kind)


def gaussian_with(key, dims, deviation, bound, split, heavy, held_as=jnp.bfloat16):
    drawn = deviation * jax.random.normal(key, dims, jnp.float32)
    if split:
        drawn = drawn * block_scale(key, dims, split, -0.22, 0.18)
    return jnp.clip(with_spikes(drawn, jax.random.fold_in(key, 3), *heavy), -bound, bound).astype(held_as)


def setup_inputs(seed: int = 0) -> dict:
    arg_keys = jax.random.split(jax.random.key(seed), 6)
    hidden = gaussian_with(arg_keys[0], (SECTIONS, TOKENS, D), 1.0, 6.0, ((0, 2), (1, 16)), (1, 2, 16, 2.0))
    gain = jnp.clip(1.0 + 0.18 * jax.random.normal(arg_keys[1], (SECTIONS, D), jnp.float32), 0.099609375, 1.8984375).astype(jnp.bfloat16)
    key_grad = centred(arg_keys[2], (SECTIONS, TOKENS, KW), 1.0, 6.0, ((0, 2), (1, 16)))
    residual_grad = centred(arg_keys[3], (SECTIONS, TOKENS, D), 0.5, 6.0, ((0, 2), (1, 16)))
    key_weight = centred(arg_keys[4], (SECTIONS, D, KW), D ** -0.5, 0.09375, ((0, 2), (1, 16)))
    return dict(hidden=hidden, gain=gain, key_grad=key_grad, residual_grad=residual_grad, key_weight=key_weight)


def one_section(hidden, gain, key_grad, residual_grad, key_weight):
    x = hidden.astype(jnp.float32)
    g = gain.astype(jnp.float32)
    scale = 1.0 / jnp.sqrt(lax.optimization_barrier(jnp.mean(x * x, axis=-1, keepdims=True)) + 1e-05)
    normed = (x * scale * g).astype(jnp.bfloat16)
    grad_w = lax.dot_general(normed, key_grad, (((0,), (0,)), ((), ())), preferred_element_type=jnp.float32)
    grad_w = grad_w / math.sqrt(TOKENS)
    normed_grad = lax.dot_general(key_grad, key_weight, (((1,), (1,)), ((), ())), preferred_element_type=jnp.float32)
    weighted = normed_grad * g
    inner = lax.optimization_barrier(jnp.mean(weighted * x, axis=-1, keepdims=True))
    input_grad = weighted * scale - x * inner * scale * scale * scale + residual_grad.astype(jnp.float32)
    return (input_grad.astype(jnp.bfloat16), grad_w)

def reference(hidden, gain, key_grad, residual_grad, key_weight):
    inputs = []
    weights = []
    for section_id in range(SECTIONS):
        got, grad_w = one_section(hidden[section_id], gain[section_id], key_grad[section_id], residual_grad[section_id], key_weight[section_id])
        inputs.append(got)
        weights.append(grad_w)
    passed = inputs[1:] + [jnp.zeros_like(inputs[0])]
    return (jnp.stack(passed), jnp.stack(weights))
```

```python
import functools
import math

import jax
import jax.numpy as jnp
from jax import lax
from jax.experimental import pallas as pl
from jax.experimental.pallas import tpu as pltpu
from jax.sharding import PartitionSpec as P

F32, BF16 = jnp.float32, jnp.bfloat16
AXES = ("section", "fsdp")
EPS = 1e-05
LANES = 128


def passed_along(x, axis, by):
    length = lax.axis_size(axis)
    pairs = [(i, i + by) for i in range(length) if 0 <= i + by < length]
    return lax.ppermute(x, axis, pairs)


def plain_body(hidden, gain, key_grad, residual_grad, key_weight):
    x = hidden[0].astype(F32)
    g = gain[0].astype(F32)
    grads = key_grad[0]
    total_tokens = hidden.shape[1] * lax.axis_size("fsdp")
    scale = 1.0 / jnp.sqrt(jnp.mean(x * x, axis=-1, keepdims=True) + EPS)
    normed = (x * scale * g).astype(BF16)
    normed_grad = lax.dot_general(
        grads,
        lax.all_gather(key_weight[0], "fsdp", axis=0, tiled=True),
        (((1,), (1,)), ((), ())),
        preferred_element_type=F32,
    )
    weighted = normed_grad * g
    inner = jnp.mean(weighted * x, axis=-1, keepdims=True)
    result = (
        weighted * scale - x * inner * scale * scale * scale + residual_grad[0].astype(F32)
    )
    passed = passed_along(result.astype(BF16), "section", -1)
    summed = lax.psum_scatter(
        lax.dot_general(normed, grads, (((0,), (0,)), ((), ())), preferred_element_type=F32),
        "fsdp",
        scatter_dimension=0,
        tiled=True,
    )
    grad_w = summed / math.sqrt(total_tokens)
    return (passed[None], grad_w[None])


def vmem(n):
    return [pl.BlockSpec(memory_space=pltpu.VMEM)] * n


SMEM = pl.BlockSpec(memory_space=pltpu.SMEM)


def cost(flops, nbytes):
    return pl.CostEstimate(flops=int(flops), bytes_accessed=int(nbytes), transcendentals=0)


def aligned(i, by):
    return pl.multiple_of(i, by)


def pack_kernel(zs, width, skip, at, h_ref, kg_ref, buf_ref, scale_ref):
    d = h_ref.shape[1]
    span = d // zs
    acc = jnp.zeros((h_ref.shape[0], LANES), F32)
    for j in range(0, d, LANES):
        v = h_ref[:, j : j + LANES].astype(F32)
        acc += v * v
    total = jnp.sum(acc, axis=1, keepdims=True)
    scale = lax.rsqrt(total / d + EPS)
    scale_ref[...] = jnp.broadcast_to(scale, scale_ref.shape)
    other = 1 - at[1]
    for k in range(zs):
        start = aligned(k * span + other * skip, LANES)
        buf_ref[:, k * width : (k + 1) * width] = h_ref[:, pl.ds(start, width)]
    end = zs * width
    kw = kg_ref.shape[1]
    buf_ref[:, end : end + kw] = kg_ref[...]
    hi = scale.astype(BF16)
    rest = scale - hi.astype(F32)
    mid = rest.astype(BF16)
    low = (rest - mid.astype(F32)).astype(BF16)
    lane = lax.broadcasted_iota(jnp.int32, (h_ref.shape[0], LANES), 1)
    parts = jnp.where(
        lane == 0, hi.astype(F32), jnp.where(lane == 1, mid.astype(F32), low.astype(F32))
    )
    buf_ref[:, end + kw :] = parts.astype(BF16)


def wgrad_kernel(
    zs, width, skip, rows, at, h_ref, kg_ref, scale_ref, buf_ref, g_ref, mine_ref, send_ref, kg2, prod
):
    t, d = h_ref.shape
    span = d // zs
    x, c = at[1], at[2]
    kw = kg_ref.shape[1]
    end = zs * width
    kg2[:t, :] = kg_ref[...]
    kg2[t:, :] = buf_ref[:, end : end + kw]
    parts = buf_ref[:, end + kw :].astype(F32)
    other_scale = parts[:, 0:1] + parts[:, 1:2] + parts[:, 2:3]
    own_scale = scale_ref[:, 0:1]
    pad = x * (2 * rows - skip)
    for k in range(zs):
        start = aligned(k * span + x * skip, LANES)
        g = g_ref[:, pl.ds(start, width)].astype(F32)
        own = (h_ref[:, pl.ds(start, width)].astype(F32) * own_scale * g).astype(BF16)
        far = (buf_ref[:, k * width : (k + 1) * width].astype(F32) * other_scale * g).astype(BF16)
        normed = jnp.concatenate([own, far], axis=0)
        prod[...] = lax.dot_general(
            normed, kg2[...], (((0,), (0,)), ((), ())), preferred_element_type=F32
        )
        mine_ref[k] = prod[pl.ds(aligned(pad + c * rows, 32), rows), :]
        send_ref[k] = prod[pl.ds(aligned(pad + (1 - c) * rows, 32), rows), :]


def split_kernel(zs, at, mine_ref, got_ref, own_ref, *out_refs):
    z = at[0]
    own_ref[...] = mine_ref[z] + got_ref[z]
    for k in range(1, zs):
        to = lax.rem(z + k, zs)
        out_refs[k - 1][...] = (mine_ref[to] + got_ref[to]).astype(BF16)


def igrad_kernel(rows, chunk, order, at, kg_ref, g_ref, h_ref, res_ref, *refs):
    n = len(order)
    pieces, (out_ref, w_ref, ng_ref) = refs[:n], refs[n:]
    t, d = h_ref.shape
    zs = n // 4
    for (dz, dx, dc), piece in zip(order, pieces):
        z = lax.rem(at[0] + zs - dz, zs)
        x = at[1] ^ dx
        c = at[2] ^ dc
        w_ref[pl.ds(aligned(((z * 2 + x) * 2 + c) * rows, 32), rows), :] = piece[...]
    dots = jnp.zeros((t, LANES), F32)
    squares = jnp.zeros((t, LANES), F32)
    kg = kg_ref[...]
    for j in range(0, d, chunk):
        ng = lax.dot_general(
            kg, w_ref[j : j + chunk, :], (((1,), (1,)), ((), ())), preferred_element_type=F32
        )
        for i in range(0, chunk, LANES):
            at_i = slice(j + i, j + i + LANES)
            v = h_ref[:, at_i].astype(F32)
            wt = ng[:, i : i + LANES] * g_ref[:, at_i].astype(F32)
            ng_ref[:, at_i] = wt
            dots += wt * v
            squares += v * v
    scale = lax.rsqrt(jnp.sum(squares, axis=1, keepdims=True) / d + EPS)
    inner = jnp.sum(dots, axis=1, keepdims=True) / d
    back = inner * scale * scale * scale
    for j in range(0, d, LANES):
        s = slice(j, j + LANES)
        out = ng_ref[:, s] * scale - h_ref[:, s].astype(F32) * back + res_ref[:, s].astype(F32)
        out_ref[:, s] = out.astype(BF16)


def staged_body(hidden, gain, key_grad, residual_grad, key_weight):
    sections, n = lax.axis_size("section"), lax.axis_size("fsdp")
    zs = n // 4
    hid, kg, res, kw = hidden[0], key_grad[0], residual_grad[0], key_weight[0]
    t, d = hid.shape
    rows, kwid = kw.shape
    own2 = 2 * rows
    skip = own2 // LANES * LANES
    width = max(-(-own2 // LANES) * LANES, 2 * own2 - skip)
    me = lax.axis_index("fsdp")
    at = jnp.stack([me // 4, me // 2 % 2, me % 2]).astype(jnp.int32)

    def move(v, to, which):
        pairs = []
        for s in which:
            for i in range(n):
                z, x, c = to(i // 4, i // 2 % 2, i % 2)
                pairs.append((s * n + i, s * n + (z * 2 + x) * 2 + c))
        return lax.ppermute(v, AXES, pairs)

    def shift(v, k, which):
        return move(v, lambda z, x, c: ((z + k) % zs, x, c), which)

    def swap_x(v, which):
        return move(v, lambda z, x, c: (z, 1 - x, c), which)

    def swap_core(v, which):
        return move(v, lambda z, x, c: (z, x, 1 - c), which)

    every = range(sections)
    later = range(1, sections)

    held = {(0, 0, 0): kw}
    for k in sorted(range(1, zs), key=lambda k: (min(k, zs - k), k)):
        held[(k, 0, 0)] = shift(kw, k, later)
    for dz in [p[0] for p in list(held)]:
        held[(dz, 1, 0)] = swap_x(held[(dz, 0, 0)], later)
    for p in list(held):
        held[(p[0], p[1], 1)] = swap_core(held[p], later)

    end = zs * width
    packed, scale = pl.pallas_call(
        functools.partial(pack_kernel, zs, width, skip),
        out_shape=(
            jax.ShapeDtypeStruct((t, end + kwid + LANES), BF16),
            jax.ShapeDtypeStruct((t, LANES), F32),
        ),
        in_specs=[SMEM] + vmem(2),
        out_specs=tuple(vmem(2)),
        cost_estimate=cost(t * d * 2, t * d * 4),
    )(at, hid, kg)
    got = swap_x(packed, every)
    mine, send = pl.pallas_call(
        functools.partial(wgrad_kernel, zs, width, skip, rows),
        out_shape=(jax.ShapeDtypeStruct((zs, rows, kwid), F32),) * 2,
        in_specs=[SMEM] + vmem(5),
        out_specs=tuple(vmem(2)),
        scratch_shapes=[pltpu.VMEM((2 * t, kwid), BF16), pltpu.VMEM((width, kwid), F32)],
        cost_estimate=cost(4 * t * end * kwid, end * kwid * 8),
    )(at, hid, kg, scale, got, gain)
    both = swap_core(send, every)
    parts = pl.pallas_call(
        functools.partial(split_kernel, zs),
        out_shape=(jax.ShapeDtypeStruct((rows, kwid), F32),)
        + (jax.ShapeDtypeStruct((rows, kwid), BF16),) * (zs - 1),
        in_specs=[SMEM] + vmem(2),
        out_specs=tuple(vmem(zs)),
        cost_estimate=cost(zs * rows * kwid, zs * rows * kwid * 10),
    )(at, mine, both)
    summed = parts[0]
    for k in range(1, zs):
        summed = summed + shift(parts[k], k, every).astype(F32)
    grad_w = summed / math.sqrt(t * n)

    order = tuple(held)
    result = pl.pallas_call(
        functools.partial(igrad_kernel, rows, math.gcd(d, 512), order),
        out_shape=jax.ShapeDtypeStruct((t, d), BF16),
        in_specs=[SMEM] + vmem(4 + len(order)),
        out_specs=vmem(1)[0],
        scratch_shapes=[pltpu.VMEM((d, kwid), BF16), pltpu.VMEM((t, d), F32)],
        cost_estimate=cost(2 * t * d * kwid, d * kwid * 4 + t * d * 8),
    )(at, kg, gain, hid, res, *[held[p] for p in order])
    passed = passed_along(result, "section", -1)
    return (passed[None], grad_w[None])


def solution(mesh):
    sections, n = mesh.shape["section"], mesh.shape["fsdp"]

    def body(*args):
        rows = args[4].shape[1]
        staged = (
            n % 4 == 0 and 2 <= n // 4 <= 8 and rows % 32 == 0 and 4 * rows % LANES == 0
            and args[0].shape[1] % 16 == 0
        )
        return (staged_body if staged else plain_body)(*args)

    return jax.shard_map(
        body,
        mesh=mesh,
        in_specs=(
            P("section", "fsdp", None),
            P("section", None),
            P("section", "fsdp", None),
            P("section", "fsdp", None),
            P("section", "fsdp", None),
        ),
        out_specs=(P("section", "fsdp", None), P("section", "fsdp", None)),
        check_vma=False,
    )
```
